32 devices in a mesh: groups: 2 (over y), section: 4 (over z), head: 4 (over x, core).
Axes of the slice: x: 2, y: 2, z: 4, core: 2. Of those that a mesh axis runs over, the one named last changes fastest.
Arguments:
- queries: bfloat16 [1024, 2048], P(('groups', 'section'), 'head'), parts along dimension 0, may hold values from -16 to 16
- token_key_rows: bfloat16 [1024, 1024], P(('groups', 'section'), 'head'), parts along dimension 0, may hold values from -16 to 16
- token_value_rows: bfloat16 [1024, 1024], P(('groups', 'section'), 'head'), parts along dimension 0, may hold values from -6 to 6
- residual: bfloat16 [1024, 5376], P(('groups', 'section', 'head')), parts along dimension 0, may hold values from -6 to 6
- prefix: int32 [8], P('groups'), parts along dimension 0, may hold values from 0 to 128, as said below
- out_weight: bfloat16 [2048, 5376], P('head', 'section'), may hold values from -1 to 1
- post_gain: float32 [5376], replicated, may hold values from 0.25 to 1.75
Outputs:
- layer_out: bfloat16 [1024, 5376], P(('groups', 'section', 'head')), parts along dimension 0
The draws below stay inside these ranges and needn't reach their ends.
There are 2 independent parts, one for each index of `groups`. The reference program is written for one: setup_inputs(seed, part) draws one part's arguments, and reference() takes and returns one part's arrays. A program takes and returns all parts, laid end to end along the dimension named above; an argument that names none is the same for every part. Nothing has to cross between parts.
Inputs may be any that keep to these rules, and one draw needn't show every extreme that they name: `prefix`: some section at index 1 or higher has the most, 128.
All inputs are finite; a program needn't handle non-finite values.
Results may differ from the reference program's by a relative error of at most 0.012.
Values may be sent and summed in bfloat16 or wider, within the bound.
A program may use at most 64 MiB of HBM per device.

```python
import jax
import jax.numpy as jnp
from jax import lax

D = 5376
HEAD_SIZE = 128
QUERY_HEADS = 16
KEY_VALUE_HEADS = 8
SECTION_ROWS = 128
SEQUENCE_TOKENS = 512
REACH = 1
N_SECTION = 4
N_HEAD = 4


def drawn_pair(key):
    starting_key = jax.random.fold_in(key, 71)
    query_tile_block = jnp.clip(jax.random.normal(jax.random.fold_in(starting_key, 8), (SEQUENCE_TOKENS, QUERY_HEADS * HEAD_SIZE), jnp.float32), -6.0, 6.0)
    key_tile_block = jnp.clip(jax.random.normal(jax.random.fold_in(starting_key, 9), (SEQUENCE_TOKENS, KEY_VALUE_HEADS * HEAD_SIZE), jnp.float32), -6.0, 6.0)
    return (query_tile_block, key_tile_block)


def draw_queries(key, part):
    return drawn_pair(key)[0].astype(jnp.bfloat16)


def draw_token_key_rows(key, part):
    return drawn_pair(key)[1].astype(jnp.bfloat16)


def draw_prefix(key, part):
    section_count = SEQUENCE_TOKENS // SECTION_ROWS
    longest = REACH * SECTION_ROWS
    lengths = jax.random.randint(jax.random.fold_in(key, 301), (section_count,), 0, longest + 1)
    chosen = jax.random.randint(jax.random.fold_in(key, 302), (), REACH, section_count)
    marked = jnp.arange(section_count, dtype=jnp.int32) == chosen
    return jnp.where(marked, longest, lengths).astype(jnp.int32)


def draw_out_weight(key, part):
    fan_in = QUERY_HEADS * HEAD_SIZE
    entries = jnp.clip(jax.random.normal(jax.random.fold_in(key, 403), (fan_in, D), jnp.float32), -6.0, 6.0)
    return (entries * fan_in ** (-0.5)).astype(jnp.bfloat16)


def level_of(key, extent, shards, least, largest):
    gain = 1.0
    for axis_at, blocks in shards:
        heights = jax.random.uniform(jax.random.fold_in(jax.random.fold_in(key, 6), axis_at), (blocks,), jnp.float32, least / len(shards), largest / len(shards))
        gain = gain * jnp.repeat(jnp.exp(heights), extent[axis_at] // blocks).reshape((-1,) + (1,) * (len(extent) - 1 - axis_at))
    return gain


def scatter_about(stream_key, shape, deviation, most, cuts=(), kind=jnp.bfloat16):
    drawn = deviation * jax.random.normal(stream_key, shape, jnp.float32)
    if cuts:
        drawn = drawn * level_of(stream_key, shape, cuts, -0.22, 0.18)
    return jnp.clip(drawn, -most, most).astype(kind)


def setup_inputs(seed: int = 0, part: int = 0) -> dict:
    streams_of = jax.random.split(jax.random.key(seed), 8)
    own_keys = jax.random.split(jax.random.fold_in(streams_of[7], part), 8)
    queries = draw_queries(jax.random.fold_in(jax.random.fold_in(streams_of[7], part), 71), part)
    token_key_rows = draw_token_key_rows(jax.random.fold_in(jax.random.fold_in(streams_of[7], part), 71), part)
    token_value_rows = scatter_about(own_keys[2], (SEQUENCE_TOKENS, KEY_VALUE_HEADS * HEAD_SIZE), 1.0, 6.0, ((0, 4), (1, 4)))
    residual = scatter_about(own_keys[3], (SEQUENCE_TOKENS, D), 1.0, 6.0, ((0, 16),))
    prefix = draw_prefix(jax.random.fold_in(jax.random.fold_in(streams_of[7], part), 71), part)
    out_weight = draw_out_weight(jax.random.fold_in(streams_of[7], 71), part)
    post_gain = jnp.clip(1.0 + 0.15 * jax.random.normal(streams_of[6], (D,), jnp.float32), 0.25, 1.75)
    return dict(queries=queries, token_key_rows=token_key_rows, token_value_rows=token_value_rows, residual=residual, prefix=prefix, out_weight=out_weight, post_gain=post_gain)


score_scale = 168.0 ** (-0.5)
norm_eps = 1e-06

def reference(queries, token_key_rows, token_value_rows, residual, prefix, out_weight, post_gain):
    reachable_blocks = 3 * N_SECTION // 8
    prefix_window_rows = (reachable_blocks + 1) * SECTION_ROWS
    group_width = QUERY_HEADS // KEY_VALUE_HEADS
    head_columns = QUERY_HEADS * HEAD_SIZE // N_HEAD
    extended_keys = jnp.concatenate([jnp.zeros((reachable_blocks * SECTION_ROWS, KEY_VALUE_HEADS * HEAD_SIZE), token_key_rows.dtype), token_key_rows], axis=0)
    extended_values = jnp.concatenate([jnp.zeros((reachable_blocks * SECTION_ROWS, KEY_VALUE_HEADS * HEAD_SIZE), token_value_rows.dtype), token_value_rows], axis=0)

    def one_section(section_at):
        first_row = (section_at * SECTION_ROWS).astype(jnp.int32)
        query_tile_block = lax.dynamic_slice_in_dim(queries, first_row, SECTION_ROWS, 0).astype(jnp.float32)
        query_tile_block = query_tile_block.reshape(SECTION_ROWS, KEY_VALUE_HEADS, group_width, HEAD_SIZE)
        key_tile_block = lax.dynamic_slice_in_dim(extended_keys, first_row, prefix_window_rows, 0).astype(jnp.float32)
        key_tile_block = key_tile_block.reshape(prefix_window_rows, KEY_VALUE_HEADS, HEAD_SIZE)
        value_tile_block = lax.dynamic_slice_in_dim(extended_values, first_row, prefix_window_rows, 0).astype(jnp.float32)
        value_tile_block = value_tile_block.reshape(prefix_window_rows, KEY_VALUE_HEADS, HEAD_SIZE)
        query_pos = first_row + jnp.arange(SECTION_ROWS, dtype=jnp.int32)
        key_pos = first_row - reachable_blocks * SECTION_ROWS + jnp.arange(prefix_window_rows, dtype=jnp.int32)
        seen_tokens = jnp.minimum(first_row, prefix[section_at])
        lower_pos = first_row - seen_tokens
        visible = (key_pos[None, :] <= query_pos[:, None]) & (key_pos[None, :] >= lower_pos)
        scores = jnp.einsum('qkgd,pkd->kgqp', query_tile_block, key_tile_block) * score_scale
        masked = jnp.where(visible, scores, -jnp.inf)
        row_max = lax.optimization_barrier(jnp.max(masked, axis=-1))
        weights = jnp.where(visible, jnp.exp(masked - row_max[..., None]), 0.0)
        denominator = lax.optimization_barrier(jnp.sum(weights, axis=-1))
        weights_low = lax.optimization_barrier(weights.astype(jnp.bfloat16))
        combined = jnp.einsum('kgqp,pkd->qkgd', weights_low.astype(jnp.float32), value_tile_block)
        attention = combined / jnp.transpose(denominator, (2, 0, 1))[..., None]
        attention = attention.reshape(SECTION_ROWS, QUERY_HEADS * HEAD_SIZE).astype(jnp.bfloat16)
        summed = jnp.zeros((SECTION_ROWS, D), jnp.float32)
        for head_at in range(N_HEAD):
            column_block = attention[:, head_at * head_columns:(head_at + 1) * head_columns]
            weight_rows = out_weight[head_at * head_columns:(head_at + 1) * head_columns]
            partial_value = jnp.dot(column_block, weight_rows, preferred_element_type=jnp.float32)
            partial_value = lax.optimization_barrier(partial_value.astype(jnp.bfloat16))
            summed = summed + partial_value.astype(jnp.float32)
        residual_block = lax.dynamic_slice_in_dim(residual, first_row, SECTION_ROWS, 0).astype(jnp.float32)
        mean_square = lax.optimization_barrier(jnp.mean(summed * summed, axis=-1, keepdims=True))
        normed = summed * lax.rsqrt(mean_square + norm_eps) * post_gain.astype(jnp.float32)[None, :]
        return (residual_block + normed).astype(jnp.bfloat16)
    section_outputs = lax.map(one_section, jnp.arange(N_SECTION, dtype=jnp.int32))
    return section_outputs.reshape(SEQUENCE_TOKENS, D)
```

```python
import functools

import jax
import jax.numpy as jnp
from jax import lax
from jax.experimental import pallas as pl
from jax.experimental.pallas import tpu as pltpu
from jax.sharding import PartitionSpec as P

HEAD_SIZE = 128


score_scale = 168.0 ** (-0.5)
floor_value = -1e30
norm_eps = 1e-06
MESH = pl.DeviceIdType.MESH


def visiting_order(n):
    return [sorted(range(n), key=lambda t: (abs(t - s), t)) for s in range(n)]


def fused_kernel(
    n,
    heads,
    prefix_ref,
    q_hbm,
    k_hbm,
    v_hbm,
    res_hbm,
    w_hbm,
    gain_hbm,
    out_ref,
    q_v,
    k_v,
    v_v,
    k_prev,
    v_prev,
    res_v,
    w_v,
    gain_v,
    attn,
    pair_send,
    pair_recv,
    mine,
    far_send,
    far_recv,
    done_send,
    done_recv,
    load_sem,
    kv_send_sem,
    kv_recv_sem,
    attn_send_sem,
    attn_recv_sem,
    pair_send_sem,
    pair_recv_sem,
    far_send_sem,
    far_recv_sem,
    done_send_sem,
    done_recv_sem,
):
    s = lax.axis_index("section")
    h = lax.axis_index("head")
    rows = q_hbm.shape[0]
    own_rows = rows // heads
    half = heads // 2
    core = lax.rem(h, 2)
    partner = h + 1 - 2 * core
    far = lax.rem(h + 2, heads)
    key_heads = k_hbm.shape[1] // HEAD_SIZE
    group_width = q_hbm.shape[1] // k_hbm.shape[1]

    def remote(source, target, send_sem, recv_sem, where):
        return pltpu.make_async_remote_copy(
            src_ref=source,
            dst_ref=target,
            send_sem=send_sem,
            recv_sem=recv_sem,
            device_id=where,
            device_id_type=MESH,
        )

    loads = [
        pltpu.make_async_copy(source, target, load_sem.at[i])
        for i, (source, target) in enumerate(
            (
                (q_hbm, q_v),
                (k_hbm, k_v),
                (v_hbm, v_v),
                (w_hbm, w_v),
                (res_hbm, res_v),
                (gain_hbm, gain_v),
            )
        )
    ]
    for load in loads:
        load.start()

    barrier = pltpu.get_barrier_semaphore()
    for step in range(1, n):
        pl.semaphore_signal(
            barrier, inc=1, device_id={"section": lax.rem(s + step, n)}, device_id_type=MESH
        )
    pl.semaphore_signal(barrier, inc=1, device_id={"head": partner}, device_id_type=MESH)
    pl.semaphore_signal(barrier, inc=1, device_id={"head": far}, device_id_type=MESH)
    pl.semaphore_wait(barrier, n + 1)

    def kv_copies():
        above = {"section": lax.rem(s + 1, n)}
        return (
            remote(k_hbm, k_prev, kv_send_sem.at[0], kv_recv_sem.at[0], above),
            remote(v_hbm, v_prev, kv_send_sem.at[1], kv_recv_sem.at[1], above),
        )

    @pl.when(s + 1 < n)
    def _():
        for copy in kv_copies():
            copy.start()

    @pl.when(s == 0)
    def _():
        k_prev[...] = jnp.zeros_like(k_prev)
        v_prev[...] = jnp.zeros_like(v_prev)

    seen = jnp.minimum(s * rows, prefix_ref[s])
    wide = group_width * rows
    q_row = lax.rem(lax.broadcasted_iota(jnp.int32, (wide, rows), 0), rows)
    k_col = lax.broadcasted_iota(jnp.int32, (wide, rows), 1)
    own_seen = k_col <= q_row
    prev_seen = k_col >= rows - seen

    for load in loads[:3]:
        load.wait()

    def head_columns(ref, at):
        return ref[:, at * HEAD_SIZE : (at + 1) * HEAD_SIZE]

    def scores_of(query, key):
        return (
            lax.dot_general(
                query, key, (((1,), (1,)), ((), ())), preferred_element_type=jnp.float32
            )
            * score_scale
        )

    queries = [
        jnp.concatenate(
            [head_columns(q_v, kh * group_width + g) for g in range(group_width)], axis=0
        )
        for kh in range(key_heads)
    ]
    own_scores = [
        jnp.where(own_seen, scores_of(queries[kh], head_columns(k_v, kh)), floor_value)
        for kh in range(key_heads)
    ]

    @pl.when(s > 0)
    def _():
        for copy in kv_copies():
            copy.wait_recv()

    for kh in range(key_heads):
        own = own_scores[kh]
        prev = jnp.where(
            prev_seen, scores_of(queries[kh], head_columns(k_prev, kh)), floor_value
        )
        top = jnp.max(jnp.maximum(own, prev), axis=-1, keepdims=True)
        own_probs = jnp.where(own_seen, jnp.exp(own - top), 0.0)
        prev_probs = jnp.where(prev_seen, jnp.exp(prev - top), 0.0)
        total = jnp.sum(own_probs + prev_probs, axis=-1, keepdims=True)
        combined = jnp.dot(
            own_probs.astype(jnp.bfloat16),
            head_columns(v_v, kh),
            preferred_element_type=jnp.float32,
        ) + jnp.dot(
            prev_probs.astype(jnp.bfloat16),
            head_columns(v_prev, kh),
            preferred_element_type=jnp.float32,
        )
        result = (combined / total).astype(jnp.bfloat16)
        for g in range(group_width):
            at = kh * group_width + g
            attn[s, :, at * HEAD_SIZE : (at + 1) * HEAD_SIZE] = result[
                g * rows : (g + 1) * rows
            ]

    def attn_copy(slot, block, target):
        return remote(
            attn.at[block],
            attn.at[block],
            attn_send_sem.at[slot],
            attn_recv_sem.at[block],
            {"section": target},
        )

    @pl.when(s + 1 < n)
    def _():
        attn_copy(0, s, s + 1).start()

    @pl.when(s > 0)
    def _():
        attn_copy(n, s, s - 1).start()

    table = visiting_order(n)

    def visited(k):
        block = table[0][k]
        for i in range(1, n):
            block = jnp.where(s == i, table[i][k], block)
        return block

    blocks = [s] + [visited(k) for k in range(1, n)]

    def onward(block):
        target = jnp.where(block < s, s + 1, s - 1)
        return target, jnp.logical_and(target >= 0, target < n)

    def pair_copy(k):
        return remote(
            pair_send.at[k],
            pair_recv.at[k],
            pair_send_sem.at[k],
            pair_recv_sem.at[k],
            {"head": partner},
        )

    def far_copy(k):
        return remote(
            far_send.at[k],
            far_recv.at[k],
            far_send_sem.at[k],
            far_recv_sem.at[k],
            {"head": far},
        )

    def done_copy(k):
        return remote(
            done_send.at[k],
            done_recv.at[s],
            done_send_sem.at[k],
            done_recv_sem.at[s],
            {"section": blocks[k]},
        )

    far_group = lax.rem(h // 2 + 1, half)
    near_group = h // 2

    def piece(block, group, side):
        start = pl.multiple_of((group * 2 + side) * own_rows, own_rows)
        return attn[block, pl.ds(start, own_rows), :]

    def multiply(k):
        block = blocks[k]
        left = jnp.concatenate(
            [
                piece(block, far_group, 1 - core),
                piece(block, near_group, 1 - core),
                piece(block, far_group, core),
                piece(block, near_group, core),
            ],
            axis=0,
        )
        product = jnp.dot(left, w_v[...], preferred_element_type=jnp.float32)
        pair_send[k] = product[: 2 * own_rows].astype(jnp.bfloat16)
        mine[k] = product[2 * own_rows :]
        pair_copy(k).start()

    def add_pair(k):
        pair_copy(k).wait_recv()
        far_send[k] = (
            mine[k, :own_rows, :] + pair_recv[k, :own_rows, :].astype(jnp.float32)
        ).astype(jnp.bfloat16)
        far_copy(k).start()

    def add_far(k):
        far_copy(k).wait_recv()
        value = (
            mine[k, own_rows:, :]
            + pair_recv[k, own_rows:, :].astype(jnp.float32)
            + far_recv[k].astype(jnp.float32)
        ).astype(jnp.bfloat16)
        if k == 0:
            done_recv[s] = value
        else:
            done_send[k] = value
            done_copy(k).start()

    for k in range(n):
        if k == 0:
            loads[3].wait()
        else:
            block = blocks[k]
            target, valid = onward(block)
            attn_copy(k, block, s).wait_recv()

            @pl.when(valid)
            def _(k=k, block=block, target=target):
                attn_copy(k, block, target).start()

        multiply(k)
        if k > 0:
            add_far(k - 1)
        add_pair(k)
    add_far(n - 1)

    loads[4].wait()
    loads[5].wait()
    for k in range(1, n):
        block = blocks[k]
        remote(
            done_send.at[k],
            done_recv.at[block],
            done_send_sem.at[k],
            done_recv_sem.at[block],
            {"section": block},
        ).wait_recv()

    width = w_hbm.shape[1]
    squares = jnp.zeros((own_rows, 1), jnp.float32)
    for i in range(n):
        value = done_recv[i].astype(jnp.float32)
        squares = squares + jnp.sum(value * value, axis=-1, keepdims=True)
    scale = lax.rsqrt(squares / (n * width) + norm_eps)
    for i in range(n):
        columns = slice(i * width, (i + 1) * width)
        normed = done_recv[i].astype(jnp.float32) * scale * gain_v[:, columns]
        out_ref[:, columns] = (res_v[:, columns].astype(jnp.float32) + normed).astype(
            out_ref.dtype
        )

    @pl.when(s + 1 < n)
    def _():
        for copy in kv_copies():
            copy.wait_send()
        attn_copy(0, s, s + 1).wait_send()

    @pl.when(s > 0)
    def _():
        attn_copy(n, s, s - 1).wait_send()

    for k in range(n):
        pair_copy(k).wait_send()
        far_copy(k).wait_send()
        if k > 0:
            done_copy(k).wait_send()
            target, valid = onward(blocks[k])

            @pl.when(valid)
            def _(k=k, target=target):
                attn_copy(k, blocks[k], target).wait_send()


def fused_local(
    n, heads, queries, token_key_rows, token_value_rows, residual, prefix, out_weight, post_gain
):
    rows = queries.shape[0]
    own_rows = rows // heads
    width = out_weight.shape[1]
    low = jnp.bfloat16
    anywhere = pl.BlockSpec(memory_space=pl.ANY)
    dma = pltpu.SemaphoreType.DMA
    gain = post_gain[None, :]
    return pl.pallas_call(
        functools.partial(fused_kernel, n, heads),
        out_shape=jax.ShapeDtypeStruct(residual.shape, residual.dtype),
        in_specs=[pl.BlockSpec(memory_space=pltpu.SMEM)] + [anywhere] * 6,
        out_specs=pl.BlockSpec(memory_space=pltpu.VMEM),
        scratch_shapes=[
            pltpu.VMEM(queries.shape, low),
            pltpu.VMEM(token_key_rows.shape, low),
            pltpu.VMEM(token_value_rows.shape, low),
            pltpu.VMEM(token_key_rows.shape, low),
            pltpu.VMEM(token_value_rows.shape, low),
            pltpu.VMEM(residual.shape, low),
            pltpu.VMEM(out_weight.shape, low),
            pltpu.VMEM(gain.shape, jnp.float32),
            pltpu.VMEM((n,) + queries.shape, low),
            pltpu.VMEM((n, 2 * own_rows, width), low),
            pltpu.VMEM((n, 2 * own_rows, width), low),
            pltpu.VMEM((n, 2 * own_rows, width), jnp.float32),
            pltpu.VMEM((n, own_rows, width), low),
            pltpu.VMEM((n, own_rows, width), low),
            pltpu.VMEM((n, own_rows, width), low),
            pltpu.VMEM((n, own_rows, width), low),
            dma((6,)),
            dma((2,)),
            dma((2,)),
            dma((n + 1,)),
            dma((n,)),
            dma((n,)),
            dma((n,)),
            dma((n,)),
            dma((n,)),
            dma((n,)),
            dma((n,)),
        ],
        compiler_params=pltpu.CompilerParams(collective_id=0, has_side_effects=True),
    )(prefix, queries, token_key_rows, token_value_rows, residual, out_weight, gain)


def shifted(value, axis, steps):
    count = lax.axis_size(axis)
    leading, last = (max(0, -steps), min(count, count - steps))
    return lax.ppermute(value, axis, [(source, source + steps) for source in range(leading, last)])


def empty_state(row_count, key_heads, group_width):
    running_max = jnp.full((key_heads, group_width, row_count), floor_value, jnp.float32)
    running_sum = jnp.zeros((key_heads, group_width, row_count), jnp.float32)
    weighted = jnp.zeros((row_count, key_heads, group_width, HEAD_SIZE), jnp.float32)
    return (running_max, running_sum, weighted)


def attend(
    status, query_tile_block, query_pos, lower_pos, key_tile_block, value_tile_block, key_pos
):
    running_max, running_sum, weighted = status
    row_count = query_tile_block.shape[0]
    key_heads = key_tile_block.shape[1] // HEAD_SIZE
    group_width = query_tile_block.shape[1] // (key_heads * HEAD_SIZE)
    query_four = query_tile_block.reshape(row_count, key_heads, group_width, HEAD_SIZE)
    key_three = key_tile_block.reshape(key_tile_block.shape[0], key_heads, HEAD_SIZE)
    value_three = value_tile_block.reshape(value_tile_block.shape[0], key_heads, HEAD_SIZE)
    scores = (
        jnp.einsum("qkgd,pkd->kgqp", query_four, key_three, preferred_element_type=jnp.float32)
        * score_scale
    )
    visible = (key_pos[None, :] <= query_pos[:, None]) & (key_pos[None, :] >= lower_pos)
    masked = jnp.where(visible, scores, floor_value)
    new_max = jnp.maximum(running_max, jnp.max(masked, axis=-1))
    carry_scale = jnp.exp(running_max - new_max)
    weights = jnp.where(visible, jnp.exp(masked - new_max[..., None]), 0.0)
    running_sum = carry_scale * running_sum + jnp.sum(weights, axis=-1)
    product = jnp.einsum(
        "kgqp,pkd->qkgd",
        weights.astype(jnp.bfloat16),
        value_three,
        preferred_element_type=jnp.float32,
    )
    weighted = jnp.transpose(carry_scale, (2, 0, 1))[..., None] * weighted + product
    return (new_max, running_sum, weighted)


def local(queries, token_key_rows, token_value_rows, residual, prefix, out_weight, post_gain):
    row_count = queries.shape[0]
    key_heads = token_key_rows.shape[1] // HEAD_SIZE
    group_width = queries.shape[1] // (key_heads * HEAD_SIZE)
    section_total = lax.axis_size("section")
    section_index = lax.axis_index("section")
    reachable_blocks = 3 * section_total // 8
    base_rows = jnp.arange(row_count, dtype=jnp.int32)
    own_pos = section_index * row_count + base_rows
    seen_tokens = jnp.minimum(section_index * row_count, prefix[section_index])
    lower_pos = section_index * row_count - seen_tokens
    block_count = (seen_tokens + row_count - 1) // row_count
    blank = empty_state(row_count, key_heads, group_width)
    states = attend(blank, queries, own_pos, lower_pos, token_key_rows, token_value_rows, own_pos)

    def process(distance, key_tile_block, value_tile_block, mine):
        key_pos = (section_index - distance) * row_count + base_rows
        use_mine = distance <= block_count
        return lax.cond(
            use_mine,
            lambda current: attend(
                current, queries, own_pos, lower_pos, key_tile_block, value_tile_block, key_pos
            ),
            lambda current: current,
            mine,
        )

    held_keys = token_key_rows[None]
    held_values = token_value_rows[None]
    stride = 1
    while stride <= reachable_blocks:
        amount_moved = min(stride, reachable_blocks + 1 - stride)
        moved_keys, moved_values = shifted(
            (held_keys[:amount_moved], held_values[:amount_moved]), "section", stride
        )
        held_keys = jnp.concatenate([held_keys, moved_keys], axis=0)
        held_values = jnp.concatenate([held_values, moved_values], axis=0)
        stride = stride * 2

    def visit_block(distance, inner):
        key_tile_block = lax.dynamic_index_in_dim(held_keys, distance, 0, keepdims=False)
        value_tile_block = lax.dynamic_index_in_dim(held_values, distance, 0, keepdims=False)
        return process(distance, key_tile_block, value_tile_block, inner)

    states = lax.fori_loop(1, reachable_blocks + 1, visit_block, states)
    attention = states[2] / jnp.transpose(states[1], (2, 0, 1))[..., None]
    attention = attention.reshape(row_count, key_heads * group_width * HEAD_SIZE).astype(
        jnp.bfloat16
    )
    partial_out = jnp.dot(
        attention,
        lax.all_gather(out_weight, "section", axis=1, tiled=True),
        preferred_element_type=jnp.float32,
    )
    summed = lax.psum_scatter(
        partial_out.astype(jnp.bfloat16), "head", scatter_dimension=0, tiled=True
    ).astype(jnp.float32)
    mean_square = jnp.mean(summed * summed, axis=-1, keepdims=True)
    normed = summed * lax.rsqrt(mean_square + norm_eps) * post_gain[None, :]
    return (residual.astype(jnp.float32) + normed).astype(jnp.bfloat16)


def solution(mesh):
    placed = (
        P(("groups", "section"), "head"),
        P(("groups", "section"), "head"),
        P(("groups", "section"), "head"),
        P(("groups", "section", "head"), None),
        P("groups"),
        P("head", "section"),
        P(),
    )
    n, heads = mesh.shape["section"], mesh.shape["head"]
    body = local
    if 3 * n // 8 == 1 and heads == 4:
        body = functools.partial(fused_local, n, heads)
    return jax.shard_map(
        body,
        mesh=mesh,
        in_specs=placed,
        out_specs=P(("groups", "section", "head"), None),
        check_vma=False,
    )
```

```python
import functools

import jax
import jax.numpy as jnp
from jax import lax
from jax.experimental import pallas as pl
from jax.experimental.pallas import tpu as pltpu
from jax.sharding import PartitionSpec as P

HEAD_SIZE = 128


score_scale = 168.0 ** (-0.5)
floor_value = -1e30
norm_eps = 1e-06
LANES = 128
CHUNKS = 2
MESH = pl.DeviceIdType.MESH


def visiting_order(n):
    return [sorted(range(n), key=lambda t: (abs(t - s), t)) for s in range(n)]


def fused_kernel(
    n,
    heads,
    chunks,
    prefix_ref,
    q_hbm,
    k_hbm,
    v_hbm,
    w_hbm,
    done_recv,
    q_v,
    k_v,
    v_v,
    k_prev,
    v_prev,
    w_v,
    attn,
    pair_send,
    pair_recv,
    mine,
    far_send,
    far_recv,
    done_send,
    load_sem,
    kv_send_sem,
    kv_recv_sem,
    attn_send_sem,
    attn_recv_sem,
    pair_send_sem,
    pair_recv_sem,
    far_send_sem,
    far_recv_sem,
    done_send_sem,
    done_recv_sem,
):
    s = lax.axis_index("section")
    h = lax.axis_index("head")
    rows = q_hbm.shape[0]
    own_rows = rows // heads
    half = heads // 2
    core = lax.rem(h, 2)
    partner = h + 1 - 2 * core
    far = lax.rem(h + 2, heads)
    key_heads = k_hbm.shape[1] // HEAD_SIZE
    group_width = q_hbm.shape[1] // k_hbm.shape[1]
    width = w_hbm.shape[0]
    edges = [LANES * round(width * c / (chunks * LANES)) for c in range(chunks)] + [width]
    spans = [slice(edges[c], edges[c + 1]) for c in range(chunks)]

    def remote(source, target, send_sem, recv_sem, where):
        return pltpu.make_async_remote_copy(
            src_ref=source,
            dst_ref=target,
            send_sem=send_sem,
            recv_sem=recv_sem,
            device_id=where,
            device_id_type=MESH,
        )

    loads = [
        pltpu.make_async_copy(source, target, load_sem.at[i])
        for i, (source, target) in enumerate(
            (
                (q_hbm, q_v),
                (k_hbm, k_v),
                (v_hbm, v_v),
                (w_hbm, w_v),
            )
        )
    ]
    for load in loads:
        load.start()

    barrier = pltpu.get_barrier_semaphore()
    for step in range(1, n):
        pl.semaphore_signal(
            barrier, inc=1, device_id={"section": lax.rem(s + step, n)}, device_id_type=MESH
        )
    pl.semaphore_signal(barrier, inc=1, device_id={"head": partner}, device_id_type=MESH)
    pl.semaphore_signal(barrier, inc=1, device_id={"head": far}, device_id_type=MESH)
    pl.semaphore_wait(barrier, n + 1)

    def kv_copies():
        above = {"section": lax.rem(s + 1, n)}
        return (
            remote(k_hbm, k_prev, kv_send_sem.at[0], kv_recv_sem.at[0], above),
            remote(v_hbm, v_prev, kv_send_sem.at[1], kv_recv_sem.at[1], above),
        )

    @pl.when(s + 1 < n)
    def _():
        for copy in kv_copies():
            copy.start()

    @pl.when(s == 0)
    def _():
        k_prev[...] = jnp.zeros_like(k_prev)
        v_prev[...] = jnp.zeros_like(v_prev)

    seen = jnp.minimum(s * rows, prefix_ref[s])
    wide = group_width * rows
    q_row = lax.rem(lax.broadcasted_iota(jnp.int32, (wide, rows), 0), rows)
    k_col = lax.broadcasted_iota(jnp.int32, (wide, rows), 1)
    own_seen = k_col <= q_row
    prev_seen = k_col >= rows - seen

    for load in loads[:3]:
        load.wait()

    def head_columns(ref, at):
        return ref[:, at * HEAD_SIZE : (at + 1) * HEAD_SIZE]

    def scores_of(query, key):
        return (
            lax.dot_general(
                query, key, (((1,), (1,)), ((), ())), preferred_element_type=jnp.float32
            )
            * score_scale
        )

    queries = [
        jnp.concatenate(
            [head_columns(q_v, kh * group_width + g) for g in range(group_width)], axis=0
        )
        for kh in range(key_heads)
    ]
    own_scores = [
        jnp.where(own_seen, scores_of(queries[kh], head_columns(k_v, kh)), floor_value)
        for kh in range(key_heads)
    ]

    @pl.when(s > 0)
    def _():
        for copy in kv_copies():
            copy.wait_recv()

    def attn_copy(slot, block, kh, target):
        return remote(
            attn.at[block, kh],
            attn.at[block, kh],
            attn_send_sem.at[slot, kh],
            attn_recv_sem.at[block, kh],
            {"section": target},
        )

    for kh in range(key_heads):
        own = own_scores[kh]
        prev = jnp.where(
            prev_seen, scores_of(queries[kh], head_columns(k_prev, kh)), floor_value
        )
        top = jnp.max(jnp.maximum(own, prev), axis=-1, keepdims=True)
        own_probs = jnp.where(own_seen, jnp.exp(own - top), 0.0)
        prev_probs = jnp.where(prev_seen, jnp.exp(prev - top), 0.0)
        total = jnp.sum(own_probs + prev_probs, axis=-1, keepdims=True)
        combined = jnp.dot(
            own_probs.astype(jnp.bfloat16),
            head_columns(v_v, kh),
            preferred_element_type=jnp.float32,
        ) + jnp.dot(
            prev_probs.astype(jnp.bfloat16),
            head_columns(v_prev, kh),
            preferred_element_type=jnp.float32,
        )
        result = (combined / total).astype(jnp.bfloat16)
        for g in range(group_width):
            attn[s, kh, :, g * HEAD_SIZE : (g + 1) * HEAD_SIZE] = result[
                g * rows : (g + 1) * rows
            ]

        @pl.when(s + 1 < n)
        def _(kh=kh):
            attn_copy(0, s, kh, s + 1).start()

        @pl.when(s > 0)
        def _(kh=kh):
            attn_copy(n, s, kh, s - 1).start()

    table = visiting_order(n)

    def visited(k):
        block = table[0][k]
        for i in range(1, n):
            block = jnp.where(s == i, table[i][k], block)
        return block

    blocks = [s] + [visited(k) for k in range(1, n)]

    def onward(block):
        target = jnp.where(block < s, s + 1, s - 1)
        return target, jnp.logical_and(target >= 0, target < n)

    def pair_copy(k, c):
        return remote(
            pair_send.at[k, :, spans[c]],
            pair_recv.at[k, :, spans[c]],
            pair_send_sem.at[k, c],
            pair_recv_sem.at[k, c],
            {"head": partner},
        )

    def far_copy(k, c):
        return remote(
            far_send.at[k, :, spans[c]],
            far_recv.at[k, :, spans[c]],
            far_send_sem.at[k, c],
            far_recv_sem.at[k, c],
            {"head": far},
        )

    def done_copy(k, c):
        return remote(
            done_send.at[k, :, spans[c]],
            done_recv.at[s, :, spans[c]],
            done_send_sem.at[k, c],
            done_recv_sem.at[s, c],
            {"section": blocks[k]},
        )

    far_group = lax.rem(h // 2 + 1, half)
    near_group = h // 2

    def piece(block, group, side):
        start = pl.multiple_of((group * 2 + side) * own_rows, own_rows)
        return jnp.concatenate(
            [attn[block, kh, pl.ds(start, own_rows), :] for kh in range(key_heads)], axis=1
        )

    def multiply(k):
        block = blocks[k]
        left = jnp.concatenate(
            [
                piece(block, far_group, 1 - core),
                piece(block, near_group, 1 - core),
                piece(block, far_group, core),
                piece(block, near_group, core),
            ],
            axis=0,
        )
        for c in range(chunks):
            product = lax.dot_general(
                left,
                w_v[spans[c], :],
                (((1,), (1,)), ((), ())),
                preferred_element_type=jnp.float32,
            )
            pair_send[k, :, spans[c]] = product[: 2 * own_rows].astype(jnp.bfloat16)
            mine[k, :, spans[c]] = product[2 * own_rows :]
            pair_copy(k, c).start()

    def add_pair(k):
        for c in range(chunks):
            span = spans[c]
            pair_copy(k, c).wait_recv()
            far_send[k, :, span] = (
                mine[k, :own_rows, span] + pair_recv[k, :own_rows, span].astype(jnp.float32)
            ).astype(jnp.bfloat16)
            far_copy(k, c).start()

    def add_far(k):
        for c in range(chunks):
            span = spans[c]
            far_copy(k, c).wait_recv()
            value = (
                mine[k, own_rows:, span]
                + pair_recv[k, own_rows:, span].astype(jnp.float32)
                + far_recv[k, :, span].astype(jnp.float32)
            ).astype(jnp.bfloat16)
            if k == 0:
                done_recv[s, :, span] = value
            else:
                done_send[k, :, span] = value
                done_copy(k, c).start()

    for k in range(n):
        if k == 0:
            loads[3].wait()
        else:
            block = blocks[k]
            target, valid = onward(block)
            for kh in range(key_heads):
                attn_copy(k, block, kh, s).wait_recv()

                @pl.when(valid)
                def _(k=k, kh=kh, block=block, target=target):
                    attn_copy(k, block, kh, target).start()

        multiply(k)
        if k > 0:
            add_far(k - 1)
        add_pair(k)
    add_far(n - 1)

    for k in range(1, n):
        block = blocks[k]
        for c in range(chunks):
            remote(
                done_send.at[k, :, spans[c]],
                done_recv.at[block, :, spans[c]],
                done_send_sem.at[k, c],
                done_recv_sem.at[block, c],
                {"section": block},
            ).wait_recv()

    @pl.when(s + 1 < n)
    def _():
        for copy in kv_copies():
            copy.wait_send()
        for kh in range(key_heads):
            attn_copy(0, s, kh, s + 1).wait_send()

    @pl.when(s > 0)
    def _():
        for kh in range(key_heads):
            attn_copy(n, s, kh, s - 1).wait_send()

    for k in range(n):
        for c in range(chunks):
            pair_copy(k, c).wait_send()
            far_copy(k, c).wait_send()
            if k > 0:
                done_copy(k, c).wait_send()
        if k > 0:
            target, valid = onward(blocks[k])

            @pl.when(valid)
            def _(k=k, target=target):
                for kh in range(key_heads):
                    attn_copy(k, blocks[k], kh, target).wait_send()


def norm_kernel(summed_ref, res_ref, gain_ref, out_ref):
    n, _, width = summed_ref.shape
    squares = 0.0
    for i in range(n):
        value = summed_ref[i].astype(jnp.float32)
        squares = squares + jnp.sum(value * value, axis=-1, keepdims=True)
    scale = lax.rsqrt(squares / (n * width) + norm_eps)
    for i in range(n):
        columns = slice(i * width, (i + 1) * width)
        normed = summed_ref[i].astype(jnp.float32) * scale * gain_ref[columns][None, :]
        out_ref[:, columns] = (res_ref[:, columns].astype(jnp.float32) + normed).astype(
            out_ref.dtype
        )


def fused_local(
    n, heads, queries, token_key_rows, token_value_rows, residual, prefix, out_weight, post_gain
):
    rows = queries.shape[0]
    own_rows = rows // heads
    width = out_weight.shape[1]
    key_heads = token_key_rows.shape[1] // HEAD_SIZE
    low = jnp.bfloat16
    anywhere = pl.BlockSpec(memory_space=pl.ANY)
    vector = pl.BlockSpec(memory_space=pltpu.VMEM)
    dma = pltpu.SemaphoreType.DMA
    weights = out_weight.T
    summed = pl.pallas_call(
        functools.partial(fused_kernel, n, heads, CHUNKS),
        out_shape=jax.ShapeDtypeStruct((n, own_rows, width), low),
        in_specs=[pl.BlockSpec(memory_space=pltpu.SMEM)] + [anywhere] * 4,
        out_specs=vector,
        scratch_shapes=[
            pltpu.VMEM(queries.shape, low),
            pltpu.VMEM(token_key_rows.shape, low),
            pltpu.VMEM(token_value_rows.shape, low),
            pltpu.VMEM(token_key_rows.shape, low),
            pltpu.VMEM(token_value_rows.shape, low),
            pltpu.VMEM(weights.shape, low),
            pltpu.VMEM((n, key_heads, rows, queries.shape[1] // key_heads), low),
            pltpu.VMEM((n, 2 * own_rows, width), low),
            pltpu.VMEM((n, 2 * own_rows, width), low),
            pltpu.VMEM((n, 2 * own_rows, width), jnp.float32),
            pltpu.VMEM((n, own_rows, width), low),
            pltpu.VMEM((n, own_rows, width), low),
            pltpu.VMEM((n, own_rows, width), low),
            dma((4,)),
            dma((2,)),
            dma((2,)),
            dma((n + 1, key_heads)),
            dma((n, key_heads)),
            dma((n, CHUNKS)),
            dma((n, CHUNKS)),
            dma((n, CHUNKS)),
            dma((n, CHUNKS)),
            dma((n, CHUNKS)),
            dma((n, CHUNKS)),
        ],
        compiler_params=pltpu.CompilerParams(collective_id=0, has_side_effects=True),
    )(prefix, queries, token_key_rows, token_value_rows, weights)
    return pl.pallas_call(
        norm_kernel,
        out_shape=jax.ShapeDtypeStruct(residual.shape, residual.dtype),
        in_specs=[vector] * 3,
        out_specs=vector,
    )(summed, residual, post_gain)


def shifted(value, axis, steps):
    count = lax.axis_size(axis)
    leading, last = (max(0, -steps), min(count, count - steps))
    return lax.ppermute(value, axis, [(source, source + steps) for source in range(leading, last)])


def empty_state(row_count, key_heads, group_width):
    running_max = jnp.full((key_heads, group_width, row_count), floor_value, jnp.float32)
    running_sum = jnp.zeros((key_heads, group_width, row_count), jnp.float32)
    weighted = jnp.zeros((row_count, key_heads, group_width, HEAD_SIZE), jnp.float32)
    return (running_max, running_sum, weighted)


def attend(
    status, query_tile_block, query_pos, lower_pos, key_tile_block, value_tile_block, key_pos
):
    running_max, running_sum, weighted = status
    row_count = query_tile_block.shape[0]
    key_heads = key_tile_block.shape[1] // HEAD_SIZE
    group_width = query_tile_block.shape[1] // (key_heads * HEAD_SIZE)
    query_four = query_tile_block.reshape(row_count, key_heads, group_width, HEAD_SIZE)
    key_three = key_tile_block.reshape(key_tile_block.shape[0], key_heads, HEAD_SIZE)
    value_three = value_tile_block.reshape(value_tile_block.shape[0], key_heads, HEAD_SIZE)
    scores = (
        jnp.einsum("qkgd,pkd->kgqp", query_four, key_three, preferred_element_type=jnp.float32)
        * score_scale
    )
    visible = (key_pos[None, :] <= query_pos[:, None]) & (key_pos[None, :] >= lower_pos)
    masked = jnp.where(visible, scores, floor_value)
    new_max = jnp.maximum(running_max, jnp.max(masked, axis=-1))
    carry_scale = jnp.exp(running_max - new_max)
    weights = jnp.where(visible, jnp.exp(masked - new_max[..., None]), 0.0)
    running_sum = carry_scale * running_sum + jnp.sum(weights, axis=-1)
    product = jnp.einsum(
        "kgqp,pkd->qkgd",
        weights.astype(jnp.bfloat16),
        value_three,
        preferred_element_type=jnp.float32,
    )
    weighted = jnp.transpose(carry_scale, (2, 0, 1))[..., None] * weighted + product
    return (new_max, running_sum, weighted)


def local(queries, token_key_rows, token_value_rows, residual, prefix, out_weight, post_gain):
    row_count = queries.shape[0]
    key_heads = token_key_rows.shape[1] // HEAD_SIZE
    group_width = queries.shape[1] // (key_heads * HEAD_SIZE)
    section_total = lax.axis_size("section")
    section_index = lax.axis_index("section")
    reachable_blocks = 3 * section_total // 8
    base_rows = jnp.arange(row_count, dtype=jnp.int32)
    own_pos = section_index * row_count + base_rows
    seen_tokens = jnp.minimum(section_index * row_count, prefix[section_index])
    lower_pos = section_index * row_count - seen_tokens
    block_count = (seen_tokens + row_count - 1) // row_count
    blank = empty_state(row_count, key_heads, group_width)
    states = attend(blank, queries, own_pos, lower_pos, token_key_rows, token_value_rows, own_pos)

    def process(distance, key_tile_block, value_tile_block, mine):
        key_pos = (section_index - distance) * row_count + base_rows
        use_mine = distance <= block_count
        return lax.cond(
            use_mine,
            lambda current: attend(
                current, queries, own_pos, lower_pos, key_tile_block, value_tile_block, key_pos
            ),
            lambda current: current,
            mine,
        )

    held_keys = token_key_rows[None]
    held_values = token_value_rows[None]
    stride = 1
    while stride <= reachable_blocks:
        amount_moved = min(stride, reachable_blocks + 1 - stride)
        moved_keys, moved_values = shifted(
            (held_keys[:amount_moved], held_values[:amount_moved]), "section", stride
        )
        held_keys = jnp.concatenate([held_keys, moved_keys], axis=0)
        held_values = jnp.concatenate([held_values, moved_values], axis=0)
        stride = stride * 2

    def visit_block(distance, inner):
        key_tile_block = lax.dynamic_index_in_dim(held_keys, distance, 0, keepdims=False)
        value_tile_block = lax.dynamic_index_in_dim(held_values, distance, 0, keepdims=False)
        return process(distance, key_tile_block, value_tile_block, inner)

    states = lax.fori_loop(1, reachable_blocks + 1, visit_block, states)
    attention = states[2] / jnp.transpose(states[1], (2, 0, 1))[..., None]
    attention = attention.reshape(row_count, key_heads * group_width * HEAD_SIZE).astype(
        jnp.bfloat16
    )
    partial_out = jnp.dot(
        attention,
        lax.all_gather(out_weight, "section", axis=1, tiled=True),
        preferred_element_type=jnp.float32,
    )
    summed = lax.psum_scatter(
        partial_out.astype(jnp.bfloat16), "head", scatter_dimension=0, tiled=True
    ).astype(jnp.float32)
    mean_square = jnp.mean(summed * summed, axis=-1, keepdims=True)
    normed = summed * lax.rsqrt(mean_square + norm_eps) * post_gain[None, :]
    return (residual.astype(jnp.float32) + normed).astype(jnp.bfloat16)


def solution(mesh):
    placed = (
        P(("groups", "section"), "head"),
        P(("groups", "section"), "head"),
        P(("groups", "section"), "head"),
        P(("groups", "section", "head"), None),
        P("groups"),
        P("head", "section"),
        P(),
    )
    n, heads = mesh.shape["section"], mesh.shape["head"]
    body = local
    if 3 * n // 8 == 1 and heads == 4:
        body = functools.partial(fused_local, n, heads)
    return jax.shard_map(
        body,
        mesh=mesh,
        in_specs=placed,
        out_specs=P(("groups", "section", "head"), None),
        check_vma=False,
    )
```

```python
import functools

import jax
import jax.numpy as jnp
from jax import lax
from jax.experimental import pallas as pl
from jax.experimental.pallas import tpu as pltpu
from jax.sharding import PartitionSpec as P

HEAD_SIZE = 128


score_scale = 168.0 ** (-0.5)
floor_value = -1e30
norm_eps = 1e-06
LANES = 128
CHUNKS = 2
VMEM_LIMIT = (60 * 1024 - 720) * 1024
MESH = pl.DeviceIdType.MESH


def visiting_order(n):
    return [sorted(range(n), key=lambda t: (abs(t - s), t)) for s in range(n)]


def plan_of(s, n):
    order = visiting_order(n)[s]
    groups = [
        [k for k in range(n) if abs(order[k] - s) == distance] for distance in range(n)
    ]
    plan, before = [], []
    for group in filter(None, groups):
        plan += [("take", k) for k in group if k]
        plan += [("multiply", k) for k in group]
        plan += [("pair", k) for k in group]
        plan += [("far", k) for k in before]
        before = group
    plan += [("far", k) for k in before]
    return tuple(plan)


def fused_kernel(
    n,
    heads,
    chunks,
    prefix_hbm,
    q_hbm,
    k_hbm,
    v_hbm,
    w_hbm,
    done_recv,
    prefix_ref,
    q_v,
    k_v,
    v_v,
    k_prev,
    v_prev,
    w_v,
    attn,
    pair_send,
    pair_recv,
    mine,
    far_send,
    far_recv,
    done_send,
    load_sem,
    kv_send_sem,
    kv_recv_sem,
    attn_send_sem,
    attn_recv_sem,
    pair_send_sem,
    pair_recv_sem,
    far_send_sem,
    far_recv_sem,
    done_send_sem,
    done_recv_sem,
):
    s = lax.axis_index("section")
    h = lax.axis_index("head")
    rows = q_hbm.shape[0]
    own_rows = rows // heads
    half = heads // 2
    core = lax.rem(h, 2)
    partner = h + 1 - 2 * core
    far = lax.rem(h + 2, heads)
    key_heads = k_hbm.shape[1] // HEAD_SIZE
    group_width = q_hbm.shape[1] // k_hbm.shape[1]
    width = w_hbm.shape[0]
    edges = [LANES * round(width * c / (chunks * LANES)) for c in range(chunks)] + [width]
    spans = [slice(edges[c], edges[c + 1]) for c in range(chunks)]

    def remote(source, target, send_sem, recv_sem, where):
        return pltpu.make_async_remote_copy(
            src_ref=source,
            dst_ref=target,
            send_sem=send_sem,
            recv_sem=recv_sem,
            device_id=where,
            device_id_type=MESH,
        )

    loads = [
        pltpu.make_async_copy(source, target, load_sem.at[i])
        for i, (source, target) in enumerate(
            (
                (q_hbm, q_v),
                (k_hbm, k_v),
                (v_hbm, v_v),
                (w_hbm, w_v),
                (prefix_hbm, prefix_ref),
            )
        )
    ]
    for load in loads:
        load.start()

    barrier = pltpu.get_barrier_semaphore()
    for step in range(1, n):
        pl.semaphore_signal(
            barrier, inc=1, device_id={"section": lax.rem(s + step, n)}, device_id_type=MESH
        )
    pl.semaphore_signal(barrier, inc=1, device_id={"head": partner}, device_id_type=MESH)
    pl.semaphore_signal(barrier, inc=1, device_id={"head": far}, device_id_type=MESH)
    pl.semaphore_wait(barrier, n + 1)

    def head_span(at):
        return slice(at * HEAD_SIZE, (at + 1) * HEAD_SIZE)

    def kv_copies(kh):
        above = {"section": lax.rem(s + 1, n)}
        span = head_span(kh)
        return [
            remote(
                source.at[:, span],
                target.at[:, span],
                kv_send_sem.at[kh, i],
                kv_recv_sem.at[kh, i],
                above,
            )
            for i, (source, target) in enumerate(((k_hbm, k_prev), (v_hbm, v_prev)))
        ]

    @pl.when(s + 1 < n)
    def _():
        for kh in range(key_heads):
            for copy in kv_copies(kh):
                copy.start()

    @pl.when(s == 0)
    def _():
        k_prev[...] = jnp.zeros_like(k_prev)
        v_prev[...] = jnp.zeros_like(v_prev)

    loads[4].wait()
    seen = jnp.minimum(s * rows, prefix_ref[s])
    wide = group_width * rows
    q_row = lax.rem(lax.broadcasted_iota(jnp.int32, (wide, rows), 0), rows)
    k_col = lax.broadcasted_iota(jnp.int32, (wide, rows), 1)
    own_seen = k_col <= q_row
    prev_seen = k_col >= rows - seen

    for load in loads[:3]:
        load.wait()

    def head_columns(ref, at):
        return ref[:, head_span(at)]

    def scores_of(query, key):
        return (
            lax.dot_general(
                query, key, (((1,), (1,)), ((), ())), preferred_element_type=jnp.float32
            )
            * score_scale
        )

    queries = [
        jnp.concatenate(
            [head_columns(q_v, kh * group_width + g) for g in range(group_width)], axis=0
        )
        for kh in range(key_heads)
    ]
    own_scores = [
        jnp.where(own_seen, scores_of(queries[kh], head_columns(k_v, kh)), floor_value)
        for kh in range(key_heads)
    ]

    def attn_copy(slot, block, kh, target):
        return remote(
            attn.at[block, kh],
            attn.at[block, kh],
            attn_send_sem.at[slot, kh],
            attn_recv_sem.at[block, kh],
            {"section": target},
        )

    for kh in range(key_heads):

        @pl.when(s > 0)
        def _(kh=kh):
            for copy in kv_copies(kh):
                copy.wait_recv()

        own = own_scores[kh]
        prev = jnp.where(
            prev_seen, scores_of(queries[kh], head_columns(k_prev, kh)), floor_value
        )
        top = jnp.max(jnp.maximum(own, prev), axis=-1, keepdims=True)
        own_probs = jnp.where(own_seen, jnp.exp(own - top), 0.0)
        prev_probs = jnp.where(prev_seen, jnp.exp(prev - top), 0.0)
        total = jnp.sum(own_probs + prev_probs, axis=-1, keepdims=True)
        combined = jnp.dot(
            own_probs.astype(jnp.bfloat16),
            head_columns(v_v, kh),
            preferred_element_type=jnp.float32,
        ) + jnp.dot(
            prev_probs.astype(jnp.bfloat16),
            head_columns(v_prev, kh),
            preferred_element_type=jnp.float32,
        )
        result = (combined / total).astype(jnp.bfloat16)
        for g in range(group_width):
            attn[s, kh, :, g * HEAD_SIZE : (g + 1) * HEAD_SIZE] = result[
                g * rows : (g + 1) * rows
            ]

        @pl.when(s + 1 < n)
        def _(kh=kh):
            attn_copy(0, s, kh, s + 1).start()

        @pl.when(s > 0)
        def _(kh=kh):
            attn_copy(n, s, kh, s - 1).start()

    table = visiting_order(n)

    def visited(k):
        block = table[0][k]
        for i in range(1, n):
            block = jnp.where(s == i, table[i][k], block)
        return block

    blocks = [s] + [visited(k) for k in range(1, n)]

    def onward(block):
        target = jnp.where(block < s, s + 1, s - 1)
        return target, jnp.logical_and(target >= 0, target < n)

    def pair_copy(k, c):
        return remote(
            pair_send.at[k, :, spans[c]],
            pair_recv.at[k, :, spans[c]],
            pair_send_sem.at[k, c],
            pair_recv_sem.at[k, c],
            {"head": partner},
        )

    def far_copy(k, c):
        return remote(
            far_send.at[k, :, spans[c]],
            far_recv.at[k, :, spans[c]],
            far_send_sem.at[k, c],
            far_recv_sem.at[k, c],
            {"head": far},
        )

    def done_copy(k, c):
        return remote(
            done_send.at[k, :, spans[c]],
            done_recv.at[s, :, spans[c]],
            done_send_sem.at[k, c],
            done_recv_sem.at[s, c],
            {"section": blocks[k]},
        )

    far_group = lax.rem(h // 2 + 1, half)
    near_group = h // 2

    def piece(block, group, side):
        start = pl.multiple_of((group * 2 + side) * own_rows, own_rows)
        return jnp.concatenate(
            [attn[block, kh, pl.ds(start, own_rows), :] for kh in range(key_heads)], axis=1
        )

    def multiply(k):
        block = blocks[k]
        left = jnp.concatenate(
            [
                piece(block, far_group, 1 - core),
                piece(block, near_group, 1 - core),
                piece(block, far_group, core),
                piece(block, near_group, core),
            ],
            axis=0,
        )
        for c in range(chunks):
            product = lax.dot_general(
                left,
                w_v[spans[c], :],
                (((1,), (1,)), ((), ())),
                preferred_element_type=jnp.float32,
            )
            pair_send[k, :, spans[c]] = product[: 2 * own_rows].astype(jnp.bfloat16)
            mine[k, :, spans[c]] = product[2 * own_rows :]
            pair_copy(k, c).start()

    def add_pair(k):
        for c in range(chunks):
            span = spans[c]
            pair_copy(k, c).wait_recv()
            far_send[k, :, span] = (
                mine[k, :own_rows, span] + pair_recv[k, :own_rows, span].astype(jnp.float32)
            ).astype(jnp.bfloat16)
            far_copy(k, c).start()

    def add_far(k):
        for c in range(chunks):
            span = spans[c]
            far_copy(k, c).wait_recv()
            value = (
                mine[k, own_rows:, span]
                + pair_recv[k, own_rows:, span].astype(jnp.float32)
                + far_recv[k, :, span].astype(jnp.float32)
            ).astype(jnp.bfloat16)
            if k == 0:
                done_recv[s, :, span] = value
            else:
                done_send[k, :, span] = value
                done_copy(k, c).start()

    def pass_on(k):
        block = blocks[k]
        target, valid = onward(block)
        for kh in range(key_heads):
            attn_copy(k, block, kh, s).wait_recv()

            @pl.when(valid)
            def _(kh=kh):
                attn_copy(k, block, kh, target).start()

    actions = {"take": pass_on, "multiply": multiply, "pair": add_pair, "far": add_far}
    loads[3].wait()
    plans = {}
    for i in range(n):
        plans.setdefault(plan_of(i, n), []).append(i)
    for plan, places in plans.items():
        chosen = s == places[0]
        for place in places[1:]:
            chosen = jnp.logical_or(chosen, s == place)

        @pl.when(chosen)
        def _(plan=plan):
            for name, k in plan:
                actions[name](k)

    for k in range(1, n):
        block = blocks[k]
        for c in range(chunks):
            remote(
                done_send.at[k, :, spans[c]],
                done_recv.at[block, :, spans[c]],
                done_send_sem.at[k, c],
                done_recv_sem.at[block, c],
                {"section": block},
            ).wait_recv()

    @pl.when(s + 1 < n)
    def _():
        for kh in range(key_heads):
            for copy in kv_copies(kh):
                copy.wait_send()
        for kh in range(key_heads):
            attn_copy(0, s, kh, s + 1).wait_send()

    @pl.when(s > 0)
    def _():
        for kh in range(key_heads):
            attn_copy(n, s, kh, s - 1).wait_send()

    for k in range(n):
        for c in range(chunks):
            pair_copy(k, c).wait_send()
            far_copy(k, c).wait_send()
            if k > 0:
                done_copy(k, c).wait_send()
        if k > 0:
            target, valid = onward(blocks[k])

            @pl.when(valid)
            def _(k=k, target=target):
                for kh in range(key_heads):
                    attn_copy(k, blocks[k], kh, target).wait_send()


def norm_kernel(summed_ref, res_ref, gain_ref, out_ref):
    n, _, width = summed_ref.shape
    squares = 0.0
    for i in range(n):
        value = summed_ref[i].astype(jnp.float32)
        squares = squares + jnp.sum(value * value, axis=-1, keepdims=True)
    scale = lax.rsqrt(squares / (n * width) + norm_eps)
    for i in range(n):
        columns = slice(i * width, (i + 1) * width)
        normed = summed_ref[i].astype(jnp.float32) * scale * gain_ref[columns][None, :]
        out_ref[:, columns] = (res_ref[:, columns].astype(jnp.float32) + normed).astype(
            out_ref.dtype
        )


def fused_local(
    n, heads, queries, token_key_rows, token_value_rows, residual, prefix, out_weight, post_gain
):
    rows = queries.shape[0]
    own_rows = rows // heads
    width = out_weight.shape[1]
    key_heads = token_key_rows.shape[1] // HEAD_SIZE
    low = jnp.bfloat16
    stays = pl.BlockSpec(memory_space=pltpu.HBM)
    vector = pl.BlockSpec(memory_space=pltpu.VMEM)
    dma = pltpu.SemaphoreType.DMA
    weights = out_weight.T
    summed = pl.pallas_call(
        functools.partial(fused_kernel, n, heads, CHUNKS),
        out_shape=jax.ShapeDtypeStruct((n, own_rows, width), low),
        in_specs=[stays] * 5,
        out_specs=vector,
        scratch_shapes=[
            pltpu.SMEM(prefix.shape, jnp.int32),
            pltpu.VMEM(queries.shape, low),
            pltpu.VMEM(token_key_rows.shape, low),
            pltpu.VMEM(token_value_rows.shape, low),
            pltpu.VMEM(token_key_rows.shape, low),
            pltpu.VMEM(token_value_rows.shape, low),
            pltpu.VMEM(weights.shape, low),
            pltpu.VMEM((n, key_heads, rows, queries.shape[1] // key_heads), low),
            pltpu.VMEM((n, 2 * own_rows, width), low),
            pltpu.VMEM((n, 2 * own_rows, width), low),
            pltpu.VMEM((n, 2 * own_rows, width), jnp.float32),
            pltpu.VMEM((n, own_rows, width), low),
            pltpu.VMEM((n, own_rows, width), low),
            pltpu.VMEM((n, own_rows, width), low),
            dma((5,)),
            dma((key_heads, 2)),
            dma((key_heads, 2)),
            dma((n + 1, key_heads)),
            dma((n, key_heads)),
            dma((n, CHUNKS)),
            dma((n, CHUNKS)),
            dma((n, CHUNKS)),
            dma((n, CHUNKS)),
            dma((n, CHUNKS)),
            dma((n, CHUNKS)),
        ],
        compiler_params=pltpu.CompilerParams(
            collective_id=0, has_side_effects=True, vmem_limit_bytes=VMEM_LIMIT
        ),
    )(prefix, queries, token_key_rows, token_value_rows, weights)
    return pl.pallas_call(
        norm_kernel,
        out_shape=jax.ShapeDtypeStruct(residual.shape, residual.dtype),
        in_specs=[vector] * 3,
        out_specs=vector,
        compiler_params=pltpu.CompilerParams(vmem_limit_bytes=16 * 2**20),
    )(summed, residual, post_gain)


def shifted(value, axis, steps):
    count = lax.axis_size(axis)
    leading, last = (max(0, -steps), min(count, count - steps))
    return lax.ppermute(value, axis, [(source, source + steps) for source in range(leading, last)])


def empty_state(row_count, key_heads, group_width):
    running_max = jnp.full((key_heads, group_width, row_count), floor_value, jnp.float32)
    running_sum = jnp.zeros((key_heads, group_width, row_count), jnp.float32)
    weighted = jnp.zeros((row_count, key_heads, group_width, HEAD_SIZE), jnp.float32)
    return (running_max, running_sum, weighted)


def attend(
    status, query_tile_block, query_pos, lower_pos, key_tile_block, value_tile_block, key_pos
):
    running_max, running_sum, weighted = status
    row_count = query_tile_block.shape[0]
    key_heads = key_tile_block.shape[1] // HEAD_SIZE
    group_width = query_tile_block.shape[1] // (key_heads * HEAD_SIZE)
    query_four = query_tile_block.reshape(row_count, key_heads, group_width, HEAD_SIZE)
    key_three = key_tile_block.reshape(key_tile_block.shape[0], key_heads, HEAD_SIZE)
    value_three = value_tile_block.reshape(value_tile_block.shape[0], key_heads, HEAD_SIZE)
    scores = (
        jnp.einsum("qkgd,pkd->kgqp", query_four, key_three, preferred_element_type=jnp.float32)
        * score_scale
    )
    visible = (key_pos[None, :] <= query_pos[:, None]) & (key_pos[None, :] >= lower_pos)
    masked = jnp.where(visible, scores, floor_value)
    new_max = jnp.maximum(running_max, jnp.max(masked, axis=-1))
    carry_scale = jnp.exp(running_max - new_max)
    weights = jnp.where(visible, jnp.exp(masked - new_max[..., None]), 0.0)
    running_sum = carry_scale * running_sum + jnp.sum(weights, axis=-1)
    product = jnp.einsum(
        "kgqp,pkd->qkgd",
        weights.astype(jnp.bfloat16),
        value_three,
        preferred_element_type=jnp.float32,
    )
    weighted = jnp.transpose(carry_scale, (2, 0, 1))[..., None] * weighted + product
    return (new_max, running_sum, weighted)


def local(queries, token_key_rows, token_value_rows, residual, prefix, out_weight, post_gain):
    row_count = queries.shape[0]
    key_heads = token_key_rows.shape[1] // HEAD_SIZE
    group_width = queries.shape[1] // (key_heads * HEAD_SIZE)
    section_total = lax.axis_size("section")
    section_index = lax.axis_index("section")
    reachable_blocks = 3 * section_total // 8
    base_rows = jnp.arange(row_count, dtype=jnp.int32)
    own_pos = section_index * row_count + base_rows
    seen_tokens = jnp.minimum(section_index * row_count, prefix[section_index])
    lower_pos = section_index * row_count - seen_tokens
    block_count = (seen_tokens + row_count - 1) // row_count
    blank = empty_state(row_count, key_heads, group_width)
    states = attend(blank, queries, own_pos, lower_pos, token_key_rows, token_value_rows, own_pos)

    def process(distance, key_tile_block, value_tile_block, mine):
        key_pos = (section_index - distance) * row_count + base_rows
        use_mine = distance <= block_count
        return lax.cond(
            use_mine,
            lambda current: attend(
                current, queries, own_pos, lower_pos, key_tile_block, value_tile_block, key_pos
            ),
            lambda current: current,
            mine,
        )

    held_keys = token_key_rows[None]
    held_values = token_value_rows[None]
    stride = 1
    while stride <= reachable_blocks:
        amount_moved = min(stride, reachable_blocks + 1 - stride)
        moved_keys, moved_values = shifted(
            (held_keys[:amount_moved], held_values[:amount_moved]), "section", stride
        )
        held_keys = jnp.concatenate([held_keys, moved_keys], axis=0)
        held_values = jnp.concatenate([held_values, moved_values], axis=0)
        stride = stride * 2

    def visit_block(distance, inner):
        key_tile_block = lax.dynamic_index_in_dim(held_keys, distance, 0, keepdims=False)
        value_tile_block = lax.dynamic_index_in_dim(held_values, distance, 0, keepdims=False)
        return process(distance, key_tile_block, value_tile_block, inner)

    states = lax.fori_loop(1, reachable_blocks + 1, visit_block, states)
    attention = states[2] / jnp.transpose(states[1], (2, 0, 1))[..., None]
    attention = attention.reshape(row_count, key_heads * group_width * HEAD_SIZE).astype(
        jnp.bfloat16
    )
    partial_out = jnp.dot(
        attention,
        lax.all_gather(out_weight, "section", axis=1, tiled=True),
        preferred_element_type=jnp.float32,
    )
    summed = lax.psum_scatter(
        partial_out.astype(jnp.bfloat16), "head", scatter_dimension=0, tiled=True
    ).astype(jnp.float32)
    mean_square = jnp.mean(summed * summed, axis=-1, keepdims=True)
    normed = summed * lax.rsqrt(mean_square + norm_eps) * post_gain[None, :]
    return (residual.astype(jnp.float32) + normed).astype(jnp.bfloat16)


def solution(mesh):
    placed = (
        P(("groups", "section"), "head"),
        P(("groups", "section"), "head"),
        P(("groups", "section"), "head"),
        P(("groups", "section", "head"), None),
        P("groups"),
        P("head", "section"),
        P(),
    )
    n, heads = mesh.shape["section"], mesh.shape["head"]
    body = local
    if 3 * n // 8 == 1 and heads == 4:
        body = functools.partial(fused_local, n, heads)
    return jax.shard_map(
        body,
        mesh=mesh,
        in_specs=placed,
        out_specs=P(("groups", "section", "head"), None),
        check_vma=False,
    )
```

```python
import functools

import jax
import jax.numpy as jnp
from jax import lax
from jax.experimental import pallas as pl
from jax.experimental.pallas import tpu as pltpu
from jax.sharding import PartitionSpec as P

HEAD_SIZE = 128


score_scale = 168.0 ** (-0.5)
floor_value = -1e30
norm_eps = 1e-06
LANES = 128
CHUNKS = 2
ROW_PARTS = 1
VMEM_LIMIT = (60 * 1024 - 720) * 1024
MESH = pl.DeviceIdType.MESH


def visiting_order(n):
    return [sorted(range(n), key=lambda t: (abs(t - s), t)) for s in range(n)]


def plan_of(s, n):
    order = visiting_order(n)[s]
    groups = [
        [k for k in range(n) if abs(order[k] - s) == distance] for distance in range(n)
    ]
    plan, before = [], []
    for group in filter(None, groups):
        plan += [("take", k) for k in group if k]
        plan += [("multiply", k) for k in group]
        plan += [("pair", k) for k in group]
        plan += [("far", k) for k in before]
        before = group
    plan += [("far", k) for k in before]
    return tuple(plan)


def fused_kernel(
    n,
    heads,
    chunks,
    prefix_hbm,
    q_hbm,
    k_hbm,
    v_hbm,
    w_hbm,
    done_recv,
    prefix_ref,
    q_v,
    k_v,
    v_v,
    k_prev,
    v_prev,
    w_v,
    attn,
    pair_send,
    pair_recv,
    mine,
    far_send,
    far_recv,
    done_send,
    load_sem,
    kv_send_sem,
    kv_recv_sem,
    attn_send_sem,
    attn_recv_sem,
    pair_send_sem,
    pair_recv_sem,
    far_send_sem,
    far_recv_sem,
    done_send_sem,
    done_recv_sem,
):
    s = lax.axis_index("section")
    h = lax.axis_index("head")
    rows = q_hbm.shape[0]
    own_rows = rows // heads
    half = heads // 2
    core = lax.rem(h, 2)
    partner = h + 1 - 2 * core
    far = lax.rem(h + 2, heads)
    key_heads = k_hbm.shape[1] // HEAD_SIZE
    group_width = q_hbm.shape[1] // k_hbm.shape[1]
    width = w_hbm.shape[0]
    edges = [LANES * round(width * c / (chunks * LANES)) for c in range(chunks)] + [width]
    spans = [slice(edges[c], edges[c + 1]) for c in range(chunks)]

    def remote(source, target, send_sem, recv_sem, where):
        return pltpu.make_async_remote_copy(
            src_ref=source,
            dst_ref=target,
            send_sem=send_sem,
            recv_sem=recv_sem,
            device_id=where,
            device_id_type=MESH,
        )

    loads = [
        pltpu.make_async_copy(source, target, load_sem.at[i])
        for i, (source, target) in enumerate(
            (
                (q_hbm, q_v),
                (k_hbm, k_v),
                (v_hbm, v_v),
                (w_hbm, w_v),
                (prefix_hbm, prefix_ref),
            )
        )
    ]
    for load in loads:
        load.start()

    barrier = pltpu.get_barrier_semaphore()
    for step in range(1, n):
        pl.semaphore_signal(
            barrier, inc=1, device_id={"section": lax.rem(s + step, n)}, device_id_type=MESH
        )
    pl.semaphore_signal(barrier, inc=1, device_id={"head": partner}, device_id_type=MESH)
    pl.semaphore_signal(barrier, inc=1, device_id={"head": far}, device_id_type=MESH)
    pl.semaphore_wait(barrier, n + 1)

    def head_span(at):
        return slice(at * HEAD_SIZE, (at + 1) * HEAD_SIZE)

    def kv_copies(kh):
        above = {"section": lax.rem(s + 1, n)}
        span = head_span(kh)
        return [
            remote(
                source.at[:, span],
                target.at[:, span],
                kv_send_sem.at[kh, i],
                kv_recv_sem.at[kh, i],
                above,
            )
            for i, (source, target) in enumerate(((k_hbm, k_prev), (v_hbm, v_prev)))
        ]

    @pl.when(s + 1 < n)
    def _():
        for kh in range(key_heads):
            for copy in kv_copies(kh):
                copy.start()

    @pl.when(s == 0)
    def _():
        k_prev[...] = jnp.zeros_like(k_prev)
        v_prev[...] = jnp.zeros_like(v_prev)

    loads[4].wait()
    seen = jnp.minimum(s * rows, prefix_ref[s])
    wide = group_width * rows
    q_row = lax.rem(lax.broadcasted_iota(jnp.int32, (wide, rows), 0), rows)
    k_col = lax.broadcasted_iota(jnp.int32, (wide, rows), 1)
    own_seen = k_col <= q_row
    prev_seen = k_col >= rows - seen

    for load in loads[:3]:
        load.wait()

    def head_columns(ref, at):
        return ref[:, head_span(at)]

    def scores_of(query, key):
        return (
            lax.dot_general(
                query, key, (((1,), (1,)), ((), ())), preferred_element_type=jnp.float32
            )
            * score_scale
        )

    queries = [
        jnp.concatenate(
            [head_columns(q_v, kh * group_width + g) for g in range(group_width)], axis=0
        )
        for kh in range(key_heads)
    ]
    own_parts = []
    for kh in range(key_heads):
        own = jnp.where(own_seen, scores_of(queries[kh], head_columns(k_v, kh)), floor_value)
        own_top = jnp.max(own, axis=-1, keepdims=True)
        own_probs = jnp.where(own_seen, jnp.exp(own - own_top), 0.0)
        own_total = jnp.sum(own_probs, axis=-1, keepdims=True)
        own_combined = jnp.dot(
            own_probs.astype(jnp.bfloat16),
            head_columns(v_v, kh),
            preferred_element_type=jnp.float32,
        )
        own_parts.append((own_top, own_total, own_combined))

    parts = [(kh, r) for kh in range(key_heads) for r in range(ROW_PARTS)]
    part_rows = rows // ROW_PARTS

    def attn_copy(slot, block, part, target):
        kh, r = parts[part]
        here = attn.at[block, kh, r * part_rows : (r + 1) * part_rows]
        return remote(
            here,
            here,
            attn_send_sem.at[slot, part],
            attn_recv_sem.at[block, part],
            {"section": target},
        )

    for kh in range(key_heads):

        @pl.when(s > 0)
        def _(kh=kh):
            for copy in kv_copies(kh):
                copy.wait_recv()

        own_top, own_total, own_combined = own_parts[kh]
        prev = jnp.where(
            prev_seen, scores_of(queries[kh], head_columns(k_prev, kh)), floor_value
        )
        top = jnp.maximum(own_top, jnp.max(prev, axis=-1, keepdims=True))
        prev_probs = jnp.where(prev_seen, jnp.exp(prev - top), 0.0)
        carry = jnp.exp(own_top - top)
        total = carry * own_total + jnp.sum(prev_probs, axis=-1, keepdims=True)
        combined = carry * own_combined + jnp.dot(
            prev_probs.astype(jnp.bfloat16),
            head_columns(v_prev, kh),
            preferred_element_type=jnp.float32,
        )
        result = (combined / total).astype(jnp.bfloat16)
        for g in range(group_width):
            attn[s, kh, :, g * HEAD_SIZE : (g + 1) * HEAD_SIZE] = result[
                g * rows : (g + 1) * rows
            ]

        ready = [part for part in range(len(parts)) if parts[part][0] == kh]

        @pl.when(s > 0)
        def _(ready=ready):
            for part in ready:
                attn_copy(n, s, part, s - 1).start()

        @pl.when(s + 1 < n)
        def _(ready=ready):
            for part in ready:
                attn_copy(0, s, part, s + 1).start()

    table = visiting_order(n)

    def visited(k):
        block = table[0][k]
        for i in range(1, n):
            block = jnp.where(s == i, table[i][k], block)
        return block

    blocks = [s] + [visited(k) for k in range(1, n)]

    def onward(block):
        target = jnp.where(block < s, s + 1, s - 1)
        return target, jnp.logical_and(target >= 0, target < n)

    def pair_copy(k, c):
        return remote(
            pair_send.at[k, :, spans[c]],
            pair_recv.at[k, :, spans[c]],
            pair_send_sem.at[k, c],
            pair_recv_sem.at[k, c],
            {"head": partner},
        )

    def far_copy(k, c):
        return remote(
            far_send.at[k, :, spans[c]],
            far_recv.at[k, :, spans[c]],
            far_send_sem.at[k, c],
            far_recv_sem.at[k, c],
            {"head": far},
        )

    def done_copy(k, c):
        return remote(
            done_send.at[k, :, spans[c]],
            done_recv.at[s, :, spans[c]],
            done_send_sem.at[k, c],
            done_recv_sem.at[s, c],
            {"section": blocks[k]},
        )

    def keep_copy(c):
        return pltpu.make_async_copy(
            done_send.at[0, :, spans[c]], done_recv.at[s, :, spans[c]], done_send_sem.at[0, c]
        )

    far_group = lax.rem(h // 2 + 1, half)
    near_group = h // 2

    def piece(block, group, side):
        start = pl.multiple_of((group * 2 + side) * own_rows, own_rows)
        return jnp.concatenate(
            [attn[block, kh, pl.ds(start, own_rows), :] for kh in range(key_heads)], axis=1
        )

    def multiply(k):
        block = blocks[k]
        left = jnp.concatenate(
            [
                piece(block, far_group, 1 - core),
                piece(block, near_group, 1 - core),
                piece(block, far_group, core),
                piece(block, near_group, core),
            ],
            axis=0,
        )
        for c in range(chunks):
            product = lax.dot_general(
                left,
                w_v[spans[c], :],
                (((1,), (1,)), ((), ())),
                preferred_element_type=jnp.float32,
            )
            pair_send[k, :, spans[c]] = product[: 2 * own_rows].astype(jnp.bfloat16)
            mine[k, :, spans[c]] = product[2 * own_rows :]
            pair_copy(k, c).start()

    def add_pair(k):
        for c in range(chunks):
            span = spans[c]
            pair_copy(k, c).wait_recv()
            far_send[k, :, span] = (
                mine[k, :own_rows, span] + pair_recv[k, :own_rows, span].astype(jnp.float32)
            ).astype(jnp.bfloat16)
            far_copy(k, c).start()

    def add_far(k):
        for c in range(chunks):
            span = spans[c]
            far_copy(k, c).wait_recv()
            value = (
                mine[k, own_rows:, span]
                + pair_recv[k, own_rows:, span].astype(jnp.float32)
                + far_recv[k, :, span].astype(jnp.float32)
            ).astype(jnp.bfloat16)
            done_send[k, :, span] = value
            if k == 0:
                keep_copy(c).start()
            else:
                done_copy(k, c).start()

    def pass_on(k):
        block = blocks[k]
        target, valid = onward(block)
        for part in range(len(parts)):
            attn_copy(k, block, part, s).wait_recv()

            @pl.when(valid)
            def _(part=part):
                attn_copy(k, block, part, target).start()

    actions = {"take": pass_on, "multiply": multiply, "pair": add_pair, "far": add_far}
    loads[3].wait()
    plans = {}
    for i in range(n):
        plans.setdefault(plan_of(i, n), []).append(i)
    for plan, places in plans.items():
        chosen = s == places[0]
        for place in places[1:]:
            chosen = jnp.logical_or(chosen, s == place)

        @pl.when(chosen)
        def _(plan=plan):
            for name, k in plan:
                actions[name](k)

    for k in range(1, n):
        block = blocks[k]
        for c in range(chunks):
            remote(
                done_send.at[k, :, spans[c]],
                done_recv.at[block, :, spans[c]],
                done_send_sem.at[k, c],
                done_recv_sem.at[block, c],
                {"section": block},
            ).wait_recv()

    @pl.when(s + 1 < n)
    def _():
        for kh in range(key_heads):
            for copy in kv_copies(kh):
                copy.wait_send()
        for part in range(len(parts)):
            attn_copy(0, s, part, s + 1).wait_send()

    @pl.when(s > 0)
    def _():
        for part in range(len(parts)):
            attn_copy(n, s, part, s - 1).wait_send()

    for k in range(n):
        for c in range(chunks):
            pair_copy(k, c).wait_send()
            far_copy(k, c).wait_send()
            if k > 0:
                done_copy(k, c).wait_send()
            else:
                keep_copy(c).wait()
        if k > 0:
            target, valid = onward(blocks[k])

            @pl.when(valid)
            def _(k=k, target=target):
                for part in range(len(parts)):
                    attn_copy(k, blocks[k], part, target).wait_send()


def norm_kernel(summed_ref, res_ref, gain_ref, out_ref):
    n, _, width = summed_ref.shape
    squares = 0.0
    for i in range(n):
        value = summed_ref[i].astype(jnp.float32)
        squares = squares + jnp.sum(value * value, axis=-1, keepdims=True)
    scale = lax.rsqrt(squares / (n * width) + norm_eps)
    for i in range(n):
        columns = slice(i * width, (i + 1) * width)
        normed = summed_ref[i].astype(jnp.float32) * scale * gain_ref[columns][None, :]
        out_ref[:, columns] = (res_ref[:, columns].astype(jnp.float32) + normed).astype(
            out_ref.dtype
        )


def fused_local(
    n, heads, queries, token_key_rows, token_value_rows, residual, prefix, out_weight, post_gain
):
    rows = queries.shape[0]
    own_rows = rows // heads
    width = out_weight.shape[1]
    key_heads = token_key_rows.shape[1] // HEAD_SIZE
    low = jnp.bfloat16
    stays = pl.BlockSpec(memory_space=pltpu.HBM)
    vector = pl.BlockSpec(memory_space=pltpu.VMEM)
    dma = pltpu.SemaphoreType.DMA
    weights = out_weight.T
    summed = pl.pallas_call(
        functools.partial(fused_kernel, n, heads, CHUNKS),
        out_shape=jax.ShapeDtypeStruct((n, own_rows, width), low),
        in_specs=[stays] * 5,
        out_specs=stays,
        scratch_shapes=[
            pltpu.SMEM(prefix.shape, jnp.int32),
            pltpu.VMEM(queries.shape, low),
            pltpu.VMEM(token_key_rows.shape, low),
            pltpu.VMEM(token_value_rows.shape, low),
            pltpu.VMEM(token_key_rows.shape, low),
            pltpu.VMEM(token_value_rows.shape, low),
            pltpu.VMEM(weights.shape, low),
            pltpu.VMEM((n, key_heads, rows, queries.shape[1] // key_heads), low),
            pltpu.VMEM((n, 2 * own_rows, width), low),
            pltpu.VMEM((n, 2 * own_rows, width), low),
            pltpu.VMEM((n, 2 * own_rows, width), jnp.float32),
            pltpu.VMEM((n, own_rows, width), low),
            pltpu.VMEM((n, own_rows, width), low),
            pltpu.VMEM((n, own_rows, width), low),
            dma((5,)),
            dma((key_heads, 2)),
            dma((key_heads, 2)),
            dma((n + 1, key_heads * ROW_PARTS)),
            dma((n, key_heads * ROW_PARTS)),
            dma((n, CHUNKS)),
            dma((n, CHUNKS)),
            dma((n, CHUNKS)),
            dma((n, CHUNKS)),
            dma((n, CHUNKS)),
            dma((n, CHUNKS)),
        ],
        compiler_params=pltpu.CompilerParams(
            collective_id=0, has_side_effects=True, vmem_limit_bytes=VMEM_LIMIT
        ),
    )(prefix, queries, token_key_rows, token_value_rows, weights)
    return pl.pallas_call(
        norm_kernel,
        out_shape=jax.ShapeDtypeStruct(residual.shape, residual.dtype),
        in_specs=[vector] * 3,
        out_specs=vector,
        compiler_params=pltpu.CompilerParams(vmem_limit_bytes=16 * 2**20),
    )(summed, residual, post_gain)


def shifted(value, axis, steps):
    count = lax.axis_size(axis)
    leading, last = (max(0, -steps), min(count, count - steps))
    return lax.ppermute(value, axis, [(source, source + steps) for source in range(leading, last)])


def empty_state(row_count, key_heads, group_width):
    running_max = jnp.full((key_heads, group_width, row_count), floor_value, jnp.float32)
    running_sum = jnp.zeros((key_heads, group_width, row_count), jnp.float32)
    weighted = jnp.zeros((row_count, key_heads, group_width, HEAD_SIZE), jnp.float32)
    return (running_max, running_sum, weighted)


def attend(
    status, query_tile_block, query_pos, lower_pos, key_tile_block, value_tile_block, key_pos
):
    running_max, running_sum, weighted = status
    row_count = query_tile_block.shape[0]
    key_heads = key_tile_block.shape[1] // HEAD_SIZE
    group_width = query_tile_block.shape[1] // (key_heads * HEAD_SIZE)
    query_four = query_tile_block.reshape(row_count, key_heads, group_width, HEAD_SIZE)
    key_three = key_tile_block.reshape(key_tile_block.shape[0], key_heads, HEAD_SIZE)
    value_three = value_tile_block.reshape(value_tile_block.shape[0], key_heads, HEAD_SIZE)
    scores = (
        jnp.einsum("qkgd,pkd->kgqp", query_four, key_three, preferred_element_type=jnp.float32)
        * score_scale
    )
    visible = (key_pos[None, :] <= query_pos[:, None]) & (key_pos[None, :] >= lower_pos)
    masked = jnp.where(visible, scores, floor_value)
    new_max = jnp.maximum(running_max, jnp.max(masked, axis=-1))
    carry_scale = jnp.exp(running_max - new_max)
    weights = jnp.where(visible, jnp.exp(masked - new_max[..., None]), 0.0)
    running_sum = carry_scale * running_sum + jnp.sum(weights, axis=-1)
    product = jnp.einsum(
        "kgqp,pkd->qkgd",
        weights.astype(jnp.bfloat16),
        value_three,
        preferred_element_type=jnp.float32,
    )
    weighted = jnp.transpose(carry_scale, (2, 0, 1))[..., None] * weighted + product
    return (new_max, running_sum, weighted)


def local(queries, token_key_rows, token_value_rows, residual, prefix, out_weight, post_gain):
    row_count = queries.shape[0]
    key_heads = token_key_rows.shape[1] // HEAD_SIZE
    group_width = queries.shape[1] // (key_heads * HEAD_SIZE)
    section_total = lax.axis_size("section")
    section_index = lax.axis_index("section")
    reachable_blocks = 3 * section_total // 8
    base_rows = jnp.arange(row_count, dtype=jnp.int32)
    own_pos = section_index * row_count + base_rows
    seen_tokens = jnp.minimum(section_index * row_count, prefix[section_index])
    lower_pos = section_index * row_count - seen_tokens
    block_count = (seen_tokens + row_count - 1) // row_count
    blank = empty_state(row_count, key_heads, group_width)
    states = attend(blank, queries, own_pos, lower_pos, token_key_rows, token_value_rows, own_pos)

    def process(distance, key_tile_block, value_tile_block, mine):
        key_pos = (section_index - distance) * row_count + base_rows
        use_mine = distance <= block_count
        return lax.cond(
            use_mine,
            lambda current: attend(
                current, queries, own_pos, lower_pos, key_tile_block, value_tile_block, key_pos
            ),
            lambda current: current,
            mine,
        )

    held_keys = token_key_rows[None]
    held_values = token_value_rows[None]
    stride = 1
    while stride <= reachable_blocks:
        amount_moved = min(stride, reachable_blocks + 1 - stride)
        moved_keys, moved_values = shifted(
            (held_keys[:amount_moved], held_values[:amount_moved]), "section", stride
        )
        held_keys = jnp.concatenate([held_keys, moved_keys], axis=0)
        held_values = jnp.concatenate([held_values, moved_values], axis=0)
        stride = stride * 2

    def visit_block(distance, inner):
        key_tile_block = lax.dynamic_index_in_dim(held_keys, distance, 0, keepdims=False)
        value_tile_block = lax.dynamic_index_in_dim(held_values, distance, 0, keepdims=False)
        return process(distance, key_tile_block, value_tile_block, inner)

    states = lax.fori_loop(1, reachable_blocks + 1, visit_block, states)
    attention = states[2] / jnp.transpose(states[1], (2, 0, 1))[..., None]
    attention = attention.reshape(row_count, key_heads * group_width * HEAD_SIZE).astype(
        jnp.bfloat16
    )
    partial_out = jnp.dot(
        attention,
        lax.all_gather(out_weight, "section", axis=1, tiled=True),
        preferred_element_type=jnp.float32,
    )
    summed = lax.psum_scatter(
        partial_out.astype(jnp.bfloat16), "head", scatter_dimension=0, tiled=True
    ).astype(jnp.float32)
    mean_square = jnp.mean(summed * summed, axis=-1, keepdims=True)
    normed = summed * lax.rsqrt(mean_square + norm_eps) * post_gain[None, :]
    return (residual.astype(jnp.float32) + normed).astype(jnp.bfloat16)


def solution(mesh):
    placed = (
        P(("groups", "section"), "head"),
        P(("groups", "section"), "head"),
        P(("groups", "section"), "head"),
        P(("groups", "section", "head"), None),
        P("groups"),
        P("head", "section"),
        P(),
    )
    n, heads = mesh.shape["section"], mesh.shape["head"]
    body = local
    if 3 * n // 8 == 1 and heads == 4:
        body = functools.partial(fused_local, n, heads)
    return jax.shard_map(
        body,
        mesh=mesh,
        in_specs=placed,
        out_specs=P(("groups", "section", "head"), None),
        check_vma=False,
    )
```
